32 devices in a mesh: phi: 4 (over y, core), eta: 8 (over z, x).
Axes of the slice: x: 2, y: 2, z: 4, core: 2. Of those that a mesh axis runs over, the one named last changes fastest.
Arguments:
- edges: bfloat16 [65536, 128], P(('phi', 'eta')), may hold values from -6 to 6
- cotangent: bfloat16 [65536, 128], P(('phi', 'eta')), may hold values from -6 to 6
- send_rows: int32 [32, 32, 32], P(('phi', 'eta')), may hold values from 0 to 2047
- send_count: int32 [32, 32], P(('phi', 'eta')), may hold values from 1 to 32, as said below
- trip_local: int32 [262144], P(('phi', 'eta')), may hold values from 0 to 2047
- trip_remote: int32 [262144], P(('phi', 'eta')), may hold values from 0 to 1023, as said below
- w_first: bfloat16 [384, 256], replicated, may hold values from -0.3125 to 0.3125
- bias_first: float32 [256], replicated, may hold values from -4 to 4
- w_second: bfloat16 [256, 128], replicated, may hold values from -0.375 to 0.375
Outputs:
- new_edges: bfloat16 [65536, 128], P(('phi', 'eta'))
- edge_grad: bfloat16 [65536, 128], P(('phi', 'eta'))
- grad_first: float32 [384, 256], replicated
- grad_bias: float32 [256], replicated
- grad_second: float32 [256, 128], replicated
The draws below stay inside these ranges and needn't reach their ends.
Inputs may be any that keep to these rules, and one draw needn't show every extreme that they name: `send_count`: some destination device has every slot live from every source. `trip_remote`: each triplet names a live slot of a source device toward its own owner.
All inputs are finite; a program needn't handle non-finite values.
Results may differ from the reference program's by a relative error of at most 0.0053.
Values may be sent and summed in bfloat16 or wider, within the bound.
A program may use at most 128 MiB of HBM per device.

```python
import jax
import jax.numpy as jnp
from jax import lax

F = 128
HID = 256
EDGE_DEV = 2048
TRIP_DEV = 8192
CAP = 32
NDEV = 32
IN = 384
EDGES = 65536
TRIPLETS = 262144


def shared_counts(key):
    first = jax.random.fold_in(key, 7)
    second = jax.random.fold_in(key, 8)
    counts = jax.random.randint(first, (NDEV, NDEV), 1, CAP + 1)
    fullest = jax.random.randint(second, (), 0, NDEV)
    counts = jnp.where(jnp.arange(NDEV)[None, :] == fullest, CAP, counts)
    return (counts.astype(jnp.int32), fullest)


def draw_send_count(key, part):
    counts, fullest = shared_counts(key)
    return counts


def draw_trip_remote(key, part):
    counts, fullest = shared_counts(key)
    source = jax.random.randint(jax.random.fold_in(key, 11), (TRIPLETS,), 0, NDEV)
    spread = jax.random.randint(jax.random.fold_in(key, 12), (TRIPLETS,), 0, 1048576)
    position = jnp.arange(TRIPLETS)
    owner = position // TRIP_DEV
    live_count = counts[source, owner]
    slot = spread % live_count
    picked = source * CAP + slot
    picked = jnp.where(position == fullest * TRIP_DEV, 0, picked)
    picked = jnp.where(position == fullest * TRIP_DEV + TRIP_DEV - 1, NDEV * CAP - 1, picked)
    return picked.astype(jnp.int32)


def with_ends(drawn, rng, smallest, high):
    shape = drawn.shape
    index_at = [jax.random.randint(jax.random.fold_in(rng, axis), (), 0, shape[axis]) for axis in range(len(shape))]
    drawn = drawn.at[tuple(index_at)].set(smallest)
    longest = shape.index(max(shape))
    index_at[longest] = (index_at[longest] + 1) % shape[longest]
    return drawn.at[tuple(index_at)].set(high)


def block_scale(rng, extent, pieces, low, largest):
    def one(axis_at, parts):
        steps = jax.random.uniform(jax.random.fold_in(jax.random.fold_in(rng, 6), axis_at), (parts,), jnp.float32, low / len(pieces), largest / len(pieces))
        return jnp.repeat(jnp.exp(steps), extent[axis_at] // parts).reshape((-1,) + (1,) * (len(extent) - axis_at - 1))

    factor_of = one(*pieces[0])
    for cut in pieces[1:]:
        factor_of = factor_of * one(*cut)
    return factor_of


def scatter_about(rng, dims, scale, reach, split=(), kind=jnp.bfloat16):
    drawn = jax.random.normal(rng, dims, jnp.float32) * scale
    if len(split) > 0:
        drawn = block_scale(rng, dims, split, -0.22, 0.18) * drawn
    return jnp.clip(drawn, min=-reach, max=reach).astype(kind)


def setup_inputs(seed: int = 0) -> dict:
    keys = jax.random.split(jax.random.key(seed), 10)
    edges = scatter_about(keys[0], (EDGES, F), 1.0, 6.0, ((0, 32),))
    cotangent = scatter_about(keys[1], (EDGES, F), 1.0, 6.0, ((0, 32),))
    send_rows = with_ends(jax.random.randint(keys[2], (NDEV, NDEV, CAP), 0, EDGE_DEV), jax.random.fold_in(keys[2], 1), 0, EDGE_DEV - 1).astype(jnp.int32)
    send_count = draw_send_count(jax.random.fold_in(keys[9], 71), 0)
    trip_local = with_ends(jax.random.randint(keys[4], (TRIPLETS,), 0, EDGE_DEV), jax.random.fold_in(keys[4], 1), 0, EDGE_DEV - 1).astype(jnp.int32)
    trip_remote = draw_trip_remote(jax.random.fold_in(keys[9], 71), 0)
    w_first = scatter_about(keys[6], (IN, HID), IN ** -0.5, 0.3125)
    bias_first = scatter_about(keys[7], (HID,), 0.7, 4.0, (), jnp.float32)
    w_second = scatter_about(keys[8], (HID, F), HID ** -0.5, 0.375)
    return {"edges": edges, "cotangent": cotangent, "send_rows": send_rows, "send_count": send_count, "trip_local": trip_local, "trip_remote": trip_remote, "w_first": w_first, "bias_first": bias_first, "w_second": w_second}


def silu_slope(pre):
    sig = jax.nn.sigmoid(pre)
    return sig * (1.0 + pre * (1.0 - sig))


def owner_terms(owner, edges, cotangent, send_rows, send_count, trip_local, trip_remote, w_first, bias_first, w_second):
    rows = send_rows[:, owner, :]
    live = jnp.arange(CAP, dtype=jnp.int32)[None, :] < send_count[:, owner][:, None]
    global_rows = (jnp.arange(NDEV, dtype=jnp.int32)[:, None] * EDGE_DEV + rows).astype(jnp.int32)
    zero = jnp.zeros((), jnp.bfloat16)
    far_lat = jnp.where(live[:, :, None], edges[global_rows], zero).reshape(NDEV * CAP, F)
    far_cot = jnp.where(live[:, :, None], cotangent[global_rows], zero).reshape(NDEV * CAP, F)
    base = (owner * EDGE_DEV).astype(jnp.int32)
    own_lat = lax.dynamic_slice_in_dim(edges, base, EDGE_DEV, 0)
    own_cot = lax.dynamic_slice_in_dim(cotangent, base, EDGE_DEV, 0)
    tstart = (owner * TRIP_DEV).astype(jnp.int32)
    local_idx = lax.dynamic_slice_in_dim(trip_local, tstart, TRIP_DEV, 0)
    remote_idx = lax.dynamic_slice_in_dim(trip_remote, tstart, TRIP_DEV, 0)
    inner = own_lat[local_idx]
    inner_cot = own_cot[local_idx]
    outer = far_lat[remote_idx]
    outer_cot = far_cot[remote_idx]
    inner_f = inner.astype(jnp.float32)
    outer_f = outer.astype(jnp.float32)
    prod = (inner_f * outer_f).astype(jnp.bfloat16)
    joined = jnp.concatenate([inner, outer, prod], axis=1)
    pre = jnp.dot(joined, w_first, preferred_element_type=jnp.float32) + bias_first
    hidden = jax.nn.silu(pre).astype(jnp.bfloat16)
    message = jnp.dot(hidden, w_second, preferred_element_type=jnp.float32)
    local_msg = jax.ops.segment_sum(message, local_idx, EDGE_DEV)
    slot_msg = jax.ops.segment_sum(message, remote_idx, NDEV * CAP)
    dmsg = (inner_cot.astype(jnp.float32) + outer_cot.astype(jnp.float32)).astype(jnp.bfloat16)
    grad_second = jnp.dot(hidden.T, dmsg, preferred_element_type=jnp.float32)
    dpre = jnp.dot(dmsg, w_second.T, preferred_element_type=jnp.float32) * silu_slope(pre)
    dpre_b = dpre.astype(jnp.bfloat16)
    grad_first = jnp.dot(joined.T, dpre_b, preferred_element_type=jnp.float32)
    grad_bias = jnp.sum(dpre, axis=0)
    dx = jnp.dot(dpre_b, w_first.T, preferred_element_type=jnp.float32)
    d_inner = dx[:, :F] + dx[:, 2 * F:] * outer_f
    d_outer = dx[:, F:2 * F] + dx[:, 2 * F:] * inner_f
    local_grad = jax.ops.segment_sum(d_inner, local_idx, EDGE_DEV)
    slot_grad = jax.ops.segment_sum(d_outer, remote_idx, NDEV * CAP)
    slots = jnp.stack([slot_msg, slot_grad], axis=1).astype(jnp.bfloat16).reshape(NDEV, CAP, 2, F)
    slots = jnp.where(live[:, :, None, None], slots, zero)
    return base, global_rows, local_msg, local_grad, slots, grad_first, grad_bias, grad_second


def reference(edges, cotangent, send_rows, send_count, trip_local, trip_remote, w_first, bias_first, w_second):
    def step(carry, owner):
        msg_total, grad_total, acc_first, acc_bias, acc_second = carry
        base, global_rows, local_msg, local_grad, slots, g_first, g_bias, g_second = owner_terms(
            owner, edges, cotangent, send_rows, send_count, trip_local, trip_remote, w_first, bias_first, w_second)
        own_rows = base + jnp.arange(EDGE_DEV, dtype=jnp.int32)
        flat_rows = global_rows.reshape(-1)
        msg_total = msg_total.at[own_rows].add(local_msg)
        msg_total = msg_total.at[flat_rows].add(slots[:, :, 0, :].astype(jnp.float32).reshape(-1, F))
        grad_total = grad_total.at[own_rows].add(local_grad)
        grad_total = grad_total.at[flat_rows].add(slots[:, :, 1, :].astype(jnp.float32).reshape(-1, F))
        return (msg_total, grad_total, acc_first + g_first, acc_bias + g_bias, acc_second + g_second), None

    start = (jnp.zeros((EDGES, F), jnp.float32), jnp.zeros((EDGES, F), jnp.float32),
             jnp.zeros((IN, HID), jnp.float32), jnp.zeros((HID,), jnp.float32), jnp.zeros((HID, F), jnp.float32))
    final, _ = lax.scan(step, start, jnp.arange(NDEV, dtype=jnp.int32))
    msg_total, grad_total, grad_first, grad_bias, grad_second = final
    new_edges = (edges.astype(jnp.float32) + msg_total).astype(jnp.bfloat16)
    edge_grad = (cotangent.astype(jnp.float32) + grad_total).astype(jnp.bfloat16)
    return (new_edges, edge_grad, grad_first, grad_bias, grad_second)
```

```python
import functools

import jax
import jax.numpy as jnp
from jax import lax
from jax.experimental import pallas as pl
from jax.experimental.pallas import tpu as pltpu
from jax.sharding import PartitionSpec as P

AXES = ("phi", "eta")
F32 = jnp.float32
BF16 = jnp.bfloat16
VMEM_LIMIT = 60 * 1024 * 1024


def dot(a, b):
    return jnp.dot(a, b, preferred_element_type=F32)


def dot_nt(a, b):
    return lax.dot_general(a, b, (((1,), (1,)), ((), ())), preferred_element_type=F32)


def dot_tn(a, b):
    return lax.dot_general(a, b, (((0,), (0,)), ((), ())), preferred_element_type=F32)


def pick_rows(idx, n):
    t = idx.shape[1]
    cols = jnp.broadcast_to(idx, (128, t)).T
    lane = lax.broadcasted_iota(jnp.int32, (t, 128), 1)
    parts = [jnp.where(cols - 128 * j == lane, 1.0, 0.0).astype(BF16) for j in range(n // 128)]
    return jnp.concatenate(parts, axis=1)


def pick_cols(idx, n, start=0):
    row = lax.broadcasted_iota(jnp.int32, (n, idx.shape[1]), 0)
    return jnp.where(row == idx - start, 1.0, 0.0).astype(BF16)


def send_kernel(rows_ref, edges_ref, cot_ref, out_ref, ec):
    width = edges_ref.shape[1]

    @pl.when(pl.program_id(0) == 0)
    def _():
        ec[:, :width] = edges_ref[...]
        ec[:, width:] = cot_ref[...]

    out_ref[...] = dot(pick_rows(rows_ref[0], ec.shape[0]), ec[...]).astype(BF16)


def main_kernel(
    loc_ref, rem_ref, edges_ref, cot_ref, arr_ref, w1_ref, b1_ref, w2_ref,
    local_ref, slot_ref, grad_ref, bias_ref,
    ec, acc_r, g1, g2,
):
    step = pl.program_id(0)
    width = edges_ref.shape[1]
    inner_n = edges_ref.shape[0]
    slots_n = arr_ref.shape[0]

    @pl.when(step == 0)
    def _():
        ec[:, :width] = edges_ref[...]
        ec[:, width:] = cot_ref[...]
        local_ref[...] = jnp.zeros_like(local_ref)
        acc_r[...] = jnp.zeros_like(acc_r)
        g1[...] = jnp.zeros_like(g1)
        g2[...] = jnp.zeros_like(g2)
        bias_ref[...] = jnp.zeros_like(bias_ref)

    loc = loc_ref[0]
    rem = rem_ref[0]
    near = dot(pick_rows(loc, inner_n), ec[...])
    far = dot(pick_rows(rem, slots_n), arr_ref[...])
    a = near[:, :width]
    b = far[:, :width]
    dm = (near[:, width:] + far[:, width:]).astype(BF16)
    x = jnp.concatenate([a.astype(BF16), b.astype(BF16), (a * b).astype(BF16)], axis=1)
    pre = dot(x, w1_ref[...]) + b1_ref[...]
    sig = 0.5 * jnp.tanh(0.5 * pre) + 0.5
    h = (pre * sig).astype(BF16)
    m = dot(h, w2_ref[...]).astype(BF16)
    dpre = dot_nt(dm, w2_ref[...]) * (sig * (1.0 + pre * (1.0 - sig)))
    dpre_b = dpre.astype(BF16)
    dx = dot_nt(dpre_b, w1_ref[...])
    dprod = dx[:, 2 * width :]
    da = (dx[:, :width] + dprod * b).astype(BF16)
    db = (dx[:, width : 2 * width] + dprod * a).astype(BF16)
    g1[...] += dot_tn(x, dpre_b)
    g2[...] += dot_tn(h, dm)
    bias_ref[...] += jnp.sum(dpre, axis=0, keepdims=True)
    local_ref[...] += dot(pick_cols(loc, inner_n), jnp.concatenate([m, da], axis=1))
    acc_r[...] += dot(pick_cols(rem, slots_n), jnp.concatenate([m, db], axis=1))

    @pl.when(step == pl.num_programs(0) - 1)
    def _():
        slot_ref[...] = acc_r[...].astype(BF16)
        n_in = g1.shape[0]
        grad_ref[:n_in, :] = g1[...].astype(BF16)
        for k in range(g2.shape[0] // width):
            grad_ref[n_in:, k * width : (k + 1) * width] = g2[k * width : (k + 1) * width, :].astype(BF16)


def final_kernel(rows_ref, ret_ref, local_ref, edges_ref, cot_ref, new_ref, grad_ref):
    tile, width = edges_ref.shape
    hot = pick_cols(rows_ref[...], tile, pl.program_id(0) * tile)
    total = local_ref[...] + dot(hot, ret_ref[...])
    new_ref[...] = (edges_ref[...].astype(F32) + total[:, :width]).astype(BF16)
    grad_ref[...] = (cot_ref[...].astype(F32) + total[:, width:]).astype(BF16)


def full(shape):
    return pl.BlockSpec(shape, lambda i: (0,) * len(shape))


def params():
    return pltpu.CompilerParams(dimension_semantics=("arbitrary",), vmem_limit_bytes=VMEM_LIMIT)


def tile_of(n, want):
    return want if n % want == 0 else n


def local(
    edges, cotangent, send_rows, send_count, trip_local, trip_remote, w_first, bias_first, w_second
):
    n_edges, width = edges.shape
    n_in, hid = w_first.shape
    ndev = lax.axis_size("phi") * lax.axis_size("eta")
    cap = send_rows.shape[2]
    slots = ndev * cap
    n_trip = trip_local.shape[0]
    live = jnp.arange(cap, dtype=jnp.int32)[None, :] < send_count[0][:, None]
    rows = jnp.where(live, send_rows[0], -1)

    st = tile_of(slots, 512)
    outgoing = pl.pallas_call(
        send_kernel,
        grid=(slots // st,),
        in_specs=[
            pl.BlockSpec((1, 1, st), lambda i: (i, 0, 0)),
            full((n_edges, width)),
            full((n_edges, width)),
        ],
        out_specs=pl.BlockSpec((st, 2 * width), lambda i: (i, 0)),
        out_shape=jax.ShapeDtypeStruct((slots, 2 * width), BF16),
        scratch_shapes=[pltpu.VMEM((n_edges, 2 * width), BF16)],
        compiler_params=params(),
        name="send_rows",
    )(rows.reshape(slots // st, 1, st), edges, cotangent)
    arrived = lax.all_to_all(outgoing, AXES, split_axis=0, concat_axis=0, tiled=True)

    tt = tile_of(n_trip, 1024)
    steps = n_trip // tt
    pack = n_in + hid * width // hid
    near_sum, slot_sum, grads, bias = pl.pallas_call(
        main_kernel,
        grid=(steps,),
        in_specs=[
            pl.BlockSpec((1, 1, tt), lambda i: (i, 0, 0)),
            pl.BlockSpec((1, 1, tt), lambda i: (i, 0, 0)),
            full((n_edges, width)),
            full((n_edges, width)),
            full((slots, 2 * width)),
            full((n_in, hid)),
            full((1, hid)),
            full((hid, width)),
        ],
        out_specs=[
            full((n_edges, 2 * width)),
            full((slots, 2 * width)),
            full((pack, hid)),
            full((1, hid)),
        ],
        out_shape=[
            jax.ShapeDtypeStruct((n_edges, 2 * width), F32),
            jax.ShapeDtypeStruct((slots, 2 * width), BF16),
            jax.ShapeDtypeStruct((pack, hid), BF16),
            jax.ShapeDtypeStruct((1, hid), F32),
        ],
        scratch_shapes=[
            pltpu.VMEM((n_edges, 2 * width), BF16),
            pltpu.VMEM((slots, 2 * width), F32),
            pltpu.VMEM((n_in, hid), F32),
            pltpu.VMEM((hid, width), F32),
        ],
        compiler_params=params(),
        name="triplets",
    )(
        trip_local.reshape(steps, 1, tt),
        trip_remote.reshape(steps, 1, tt),
        edges,
        cotangent,
        arrived,
        w_first,
        bias_first.reshape(1, hid),
        w_second,
    )

    share = pack // ndev
    payload = jnp.concatenate(
        [slot_sum.reshape(ndev, cap, 2 * width), grads.reshape(ndev, share, hid)], axis=1
    )
    back = lax.all_to_all(payload, AXES, split_axis=0, concat_axis=0, tiled=True)
    returned = back[:, :cap].reshape(slots, 2 * width)
    part = jnp.sum(back[:, cap:].astype(F32), axis=0)
    gathered = lax.all_gather(jnp.concatenate([part, bias], axis=0), AXES)
    packed = gathered[:, :share].reshape(pack, hid)
    grad_first = packed[:n_in]
    grad_second = jnp.concatenate(
        [packed[n_in:, k * width : (k + 1) * width] for k in range(hid // width)], axis=0
    )
    grad_bias = jnp.sum(gathered[:, share], axis=0)

    et = tile_of(n_edges, 512)
    row_block = lambda w: pl.BlockSpec((et, w), lambda i: (i, 0))
    new_edges, edge_grad = pl.pallas_call(
        final_kernel,
        grid=(n_edges // et,),
        in_specs=[
            full((1, slots)),
            full((slots, 2 * width)),
            row_block(2 * width),
            row_block(width),
            row_block(width),
        ],
        out_specs=[row_block(width), row_block(width)],
        out_shape=[jax.ShapeDtypeStruct((n_edges, width), BF16)] * 2,
        compiler_params=params(),
        name="add_up",
    )(rows.reshape(1, slots), returned, near_sum, edges, cotangent)
    return (new_edges, edge_grad, grad_first, grad_bias, grad_second)


def solution(mesh):
    spec = P(AXES, None)
    in_specs = (spec, spec, P(AXES, None, None), spec, P(AXES), P(AXES), P(), P(), P())
    out_specs = (spec, spec, P(), P(), P())
    return jax.shard_map(local, mesh=mesh, in_specs=in_specs, out_specs=out_specs, check_vma=False)
```

```python
import functools

import jax
import jax.numpy as jnp
from jax import lax
from jax.experimental import pallas as pl
from jax.experimental.pallas import tpu as pltpu
from jax.sharding import PartitionSpec as P

AXES = ("phi", "eta")
F32 = jnp.float32
BF16 = jnp.bfloat16
VMEM_LIMIT = 60 * 1024 * 1024


def dot(a, b):
    return jnp.dot(a, b, preferred_element_type=F32)


def dot_nt(a, b):
    return lax.dot_general(a, b, (((1,), (1,)), ((), ())), preferred_element_type=F32)


def dot_tn(a, b):
    return lax.dot_general(a, b, (((0,), (0,)), ((), ())), preferred_element_type=F32)


def pick_rows(idx, n):
    t = idx.shape[1]
    cols = jnp.broadcast_to(idx, (128, t)).T
    lane = lax.broadcasted_iota(jnp.int32, (t, 128), 1)
    parts = [jnp.where(cols - 128 * j == lane, 1.0, 0.0).astype(BF16) for j in range(n // 128)]
    return jnp.concatenate(parts, axis=1)


def pick_cols(idx, n, start=0):
    row = lax.broadcasted_iota(jnp.int32, (n, idx.shape[1]), 0)
    return jnp.where(row == idx - start, 1.0, 0.0).astype(BF16)


def send_kernel(rows_ref, edges_ref, cot_ref, out_ref, ec):
    width = edges_ref.shape[1]

    @pl.when(pl.program_id(0) == 0)
    def _():
        ec[:, :width] = edges_ref[...]
        ec[:, width:] = cot_ref[...]

    out_ref[...] = dot(pick_rows(rows_ref[0], ec.shape[0]), ec[...]).astype(BF16)


def near_kernel(loc_ref, edges_ref, cot_ref, out_ref, ec):
    width = edges_ref.shape[1]

    @pl.when(pl.program_id(0) == 0)
    def _():
        ec[:, :width] = edges_ref[...]
        ec[:, width:] = cot_ref[...]

    out_ref[...] = dot(pick_rows(loc_ref[0], ec.shape[0]), ec[...]).astype(BF16)


def main_kernel(
    fused, rem_ref, near_ref, arr_ref, w1_ref, b1_ref, w2_ref,
    mda_ref, slot_ref, grad_ref, bias_ref,
    acc_r, g1, g2,
):
    step = pl.program_id(0)
    width = w2_ref.shape[1]
    slots_n = arr_ref.shape[0]

    @pl.when(step == 0)
    def _():
        acc_r[...] = jnp.zeros_like(acc_r)
        g1[...] = jnp.zeros_like(g1)
        g2[...] = jnp.zeros_like(g2)
        bias_ref[...] = jnp.zeros_like(bias_ref)

    rem = rem_ref[0]
    far = dot(pick_rows(rem, slots_n), arr_ref[...])
    a_b = near_ref[:, :width]
    a = a_b.astype(F32)
    b = far[:, :width]
    dm = (near_ref[:, width:].astype(F32) + far[:, width:]).astype(BF16)
    x = jnp.concatenate([a_b, b.astype(BF16), (a * b).astype(BF16)], axis=1)
    pre = dot(x, w1_ref[...]) + b1_ref[...]
    sig = 0.5 * jnp.tanh(0.5 * pre) + 0.5
    h = (pre * sig).astype(BF16)
    m = dot(h, w2_ref[...]).astype(BF16)
    dpre = dot_nt(dm, w2_ref[...]) * (sig * (1.0 + pre * (1.0 - sig)))
    dpre_b = dpre.astype(BF16)
    dx = dot_nt(dpre_b, w1_ref[...])
    dprod = dx[:, 2 * width :]
    mda_ref[:, :width] = m
    mda_ref[:, width:] = (dx[:, :width] + dprod * b).astype(BF16)
    db = (dx[:, width : 2 * width] + dprod * a).astype(BF16)
    g1[...] += dot_tn(x, dpre_b)
    g2[...] += dot_tn(h, dm)
    bias_ref[...] += jnp.sum(dpre, axis=0, keepdims=True)
    acc_r[...] += dot(pick_cols(rem, slots_n), jnp.concatenate([m, db], axis=1))

    @pl.when(step == pl.num_programs(0) - 1)
    def _():
        second = jnp.concatenate(
            [g2[k * width : (k + 1) * width, :] for k in range(g2.shape[0] // width)], axis=1
        )
        if fused:
            ndev, both, wide = slot_ref.shape
            cap = slots_n // ndev
            share = both - cap
            slot_ref[:, :cap, :] = acc_r[...].astype(BF16).reshape(ndev, cap, wide)
            split = g1.shape[0] // share
            slot_ref[:split, cap:, :] = g1[...].astype(BF16).reshape(split, share, wide)
            slot_ref[split:, cap:, :] = second.astype(BF16).reshape(ndev - split, share, wide)
            grad_ref[...] = jnp.zeros_like(grad_ref)
        else:
            n_in = g1.shape[0]
            slot_ref[...] = acc_r[...].astype(BF16)
            grad_ref[:n_in, :] = g1[...].astype(BF16)
            grad_ref[n_in:, :] = second.astype(BF16)


def scatter_kernel(loc_ref, mda_ref, out_ref):
    @pl.when(pl.program_id(0) == 0)
    def _():
        out_ref[...] = jnp.zeros_like(out_ref)

    out_ref[...] += dot(pick_cols(loc_ref[0], out_ref.shape[0]), mda_ref[...])


def gather_kernel(
    n_phi, n_eta, back_ref, bias_ref, out_ref, outb_ref, buf, bufb, send_sem, recv_sem, send_b, recv_b
):
    phi = lax.axis_index("phi")
    eta = lax.axis_index("eta")
    me = phi * n_eta + eta
    pairs = n_phi // 2
    cap = back_ref.shape[1] - buf.shape[1]
    buf[me] = jnp.sum(back_ref[:, cap:, :].astype(F32), axis=0).astype(BF16)
    bufb[me] = bias_ref[...]
    row = [(phi, lax.rem(eta + k, n_eta)) for k in range(1, n_eta)]
    column = [(lax.rem(phi + 2 * k, n_phi), eta) for k in range(1, pairs)]
    mate = (phi + 1 - 2 * lax.rem(phi, 2), eta)

    barrier = pltpu.get_barrier_semaphore()
    peers = row + column + [mate]
    for peer in peers:
        pl.semaphore_signal(barrier, inc=1, device_id=peer, device_id_type=pl.DeviceIdType.MESH)
    pl.semaphore_wait(barrier, len(peers))

    slot = 0
    for stage in range(3):
        if stage == 0:
            moves = [(peer, me, 1) for peer in row]
        elif stage == 1:
            moves = [(peer, phi * n_eta, n_eta) for peer in column]
        else:
            own = lax.rem(phi, 2)
            moves = [(mate, (own + 2 * k) * n_eta, n_eta) for k in range(pairs)]
        copies = []
        for peer, start, count in moves:
            for data, sends, recvs in ((buf, send_sem, recv_sem), (bufb, send_b, recv_b)):
                part = data.at[pl.ds(start, count)]
                copies.append(
                    pltpu.make_async_remote_copy(
                        src_ref=part,
                        dst_ref=part,
                        send_sem=sends.at[slot],
                        recv_sem=recvs.at[slot],
                        device_id=peer,
                        device_id_type=pl.DeviceIdType.MESH,
                    )
                )
            slot += 1
        for copy in copies:
            copy.start()
        for copy in copies:
            copy.wait()
    out_ref[...] = buf[...]
    outb_ref[...] = bufb[...]


def final_kernel(
    rows_ref, back_ref, local_ref, edges_ref, cot_ref, pack_ref, bias_ref,
    new_ref, grad_ref, g1_ref, g2_ref, gb_ref,
):
    tile, width = edges_ref.shape
    ndev = back_ref.shape[0]
    slots = rows_ref.shape[1]
    hot = pick_cols(rows_ref[...], tile, pl.program_id(0) * tile)
    returned = back_ref[:, : slots // ndev, :].reshape(slots, 2 * width)
    total = local_ref[...] + dot(hot, returned)
    new_ref[...] = (edges_ref[...].astype(F32) + total[:, :width]).astype(BF16)
    grad_ref[...] = (cot_ref[...].astype(F32) + total[:, width:]).astype(BF16)

    @pl.when(pl.program_id(0) == 0)
    def _():
        n_in = g1_ref.shape[0]
        g1_ref[...] = pack_ref[:n_in, :].astype(F32)
        for k in range(g2_ref.shape[0] // width):
            g2_ref[k * width : (k + 1) * width, :] = pack_ref[n_in:, k * width : (k + 1) * width].astype(F32)
        gb_ref[...] = jnp.sum(bias_ref[...], axis=0)


def full(shape):
    return pl.BlockSpec(shape, lambda i: (0,) * len(shape))


def params():
    return pltpu.CompilerParams(dimension_semantics=("arbitrary",), vmem_limit_bytes=VMEM_LIMIT)


def tile_of(n, want):
    return want if n % want == 0 else n


def local(
    edges, cotangent, send_rows, send_count, trip_local, trip_remote, w_first, bias_first, w_second
):
    n_edges, width = edges.shape
    n_in, hid = w_first.shape
    ndev = lax.axis_size("phi") * lax.axis_size("eta")
    cap = send_rows.shape[2]
    slots = ndev * cap
    n_trip = trip_local.shape[0]
    live = jnp.arange(cap, dtype=jnp.int32)[None, :] < send_count[0][:, None]
    rows = jnp.where(live, send_rows[0], -1)

    st = tile_of(slots, 512)
    outgoing = pl.pallas_call(
        send_kernel,
        grid=(slots // st,),
        in_specs=[
            pl.BlockSpec((1, 1, st), lambda i: (i, 0, 0)),
            full((n_edges, width)),
            full((n_edges, width)),
        ],
        out_specs=pl.BlockSpec((st, 2 * width), lambda i: (i, 0)),
        out_shape=jax.ShapeDtypeStruct((slots, 2 * width), BF16),
        scratch_shapes=[pltpu.VMEM((n_edges, 2 * width), BF16)],
        compiler_params=params(),
        name="send_rows",
    )(rows.reshape(slots // st, 1, st), edges, cotangent)
    arrived = lax.all_to_all(outgoing, AXES, split_axis=0, concat_axis=0, tiled=True)

    tt = tile_of(n_trip, 1024)
    steps = n_trip // tt
    wide = 2 * width
    pack = n_in + width
    share = pack // ndev
    loc = trip_local.reshape(steps, 1, tt)
    rem = trip_remote.reshape(steps, 1, tt)
    idx_block = pl.BlockSpec((1, 1, tt), lambda i: (i, 0, 0))
    trip_block = pl.BlockSpec((tt, wide), lambda i: (i, 0))
    near = pl.pallas_call(
        near_kernel,
        grid=(steps,),
        in_specs=[idx_block, full((n_edges, width)), full((n_edges, width))],
        out_specs=trip_block,
        out_shape=jax.ShapeDtypeStruct((n_trip, wide), BF16),
        scratch_shapes=[pltpu.VMEM((n_edges, wide), BF16)],
        compiler_params=params(),
        cost_estimate=pl.CostEstimate(
            flops=2 * n_trip * n_edges * wide, bytes_accessed=2 * n_trip * wide, transcendentals=0
        ),
        name="near_rows",
    )(loc, edges, cotangent)

    fused = share % 16 == 0 and n_in % share == 0 and cap % 16 == 0
    if fused:
        slot_shape, grad_shape = (ndev, cap + share, wide), (8, hid)
    else:
        slot_shape, grad_shape = (slots, wide), (pack, hid)
    mda, payload, grads, bias = pl.pallas_call(
        functools.partial(main_kernel, fused),
        grid=(steps,),
        in_specs=[
            idx_block,
            trip_block,
            full((slots, wide)),
            full((n_in, hid)),
            full((1, hid)),
            full((hid, width)),
        ],
        out_specs=[trip_block, full(slot_shape), full(grad_shape), full((1, hid))],
        out_shape=[
            jax.ShapeDtypeStruct((n_trip, wide), BF16),
            jax.ShapeDtypeStruct(slot_shape, BF16),
            jax.ShapeDtypeStruct(grad_shape, BF16),
            jax.ShapeDtypeStruct((1, hid), F32),
        ],
        scratch_shapes=[
            pltpu.VMEM((slots, wide), F32),
            pltpu.VMEM((n_in, hid), F32),
            pltpu.VMEM((hid, width), F32),
        ],
        compiler_params=params(),
        cost_estimate=pl.CostEstimate(
            flops=12 * n_trip * n_in * hid, bytes_accessed=8 * n_trip * wide, transcendentals=0
        ),
        name="triplets",
    )(rem, near, arrived, w_first, bias_first.reshape(1, hid), w_second)
    if not fused:
        payload = jnp.concatenate(
            [payload.reshape(ndev, cap, wide), grads.reshape(ndev, share, hid)], axis=1
        )
    back = lax.all_to_all(payload, AXES, split_axis=0, concat_axis=0, tiled=True)

    near_sum = pl.pallas_call(
        scatter_kernel,
        grid=(steps,),
        in_specs=[idx_block, trip_block],
        out_specs=full((n_edges, wide)),
        out_shape=jax.ShapeDtypeStruct((n_edges, wide), F32),
        compiler_params=params(),
        cost_estimate=pl.CostEstimate(
            flops=2 * n_trip * n_edges * wide, bytes_accessed=2 * n_trip * wide, transcendentals=0
        ),
        name="near_sum",
    )(loc, mda)

    n_phi, n_eta = lax.axis_size("phi"), lax.axis_size("eta")
    moves = n_eta - 1 + n_phi // 2 - 1 + n_phi // 2
    sems = pltpu.SemaphoreType.DMA((moves,))
    packed, biases = pl.pallas_call(
        functools.partial(gather_kernel, n_phi, n_eta),
        in_specs=[pl.BlockSpec(memory_space=pltpu.VMEM)] * 2,
        out_specs=[pl.BlockSpec(memory_space=pltpu.VMEM)] * 2,
        out_shape=[
            jax.ShapeDtypeStruct((ndev, share, hid), BF16),
            jax.ShapeDtypeStruct((ndev, 1, hid), F32),
        ],
        scratch_shapes=[
            pltpu.VMEM((ndev, share, hid), BF16),
            pltpu.VMEM((ndev, 1, hid), F32),
            sems,
            sems,
            sems,
            sems,
        ],
        compiler_params=pltpu.CompilerParams(
            collective_id=0, has_side_effects=True, vmem_limit_bytes=VMEM_LIMIT
        ),
        name="gather_grads",
    )(back, bias)

    et = tile_of(n_edges, 512)
    row_block = lambda w: pl.BlockSpec((et, w), lambda i: (i, 0))
    new_edges, edge_grad, grad_first, grad_second, grad_bias = pl.pallas_call(
        final_kernel,
        grid=(n_edges // et,),
        in_specs=[
            full((1, slots)),
            full((ndev, cap + share, wide)),
            row_block(wide),
            row_block(width),
            row_block(width),
            full((pack, hid)),
            full((ndev, 1, hid)),
        ],
        out_specs=[
            row_block(width),
            row_block(width),
            full((n_in, hid)),
            full((hid, width)),
            full((1, hid)),
        ],
        out_shape=[
            jax.ShapeDtypeStruct((n_edges, width), BF16),
            jax.ShapeDtypeStruct((n_edges, width), BF16),
            jax.ShapeDtypeStruct((n_in, hid), F32),
            jax.ShapeDtypeStruct((hid, width), F32),
            jax.ShapeDtypeStruct((1, hid), F32),
        ],
        compiler_params=params(),
        name="add_up",
    )(rows.reshape(1, slots), back, near_sum, edges, cotangent, packed.reshape(pack, hid), biases)
    return (new_edges, edge_grad, grad_first, grad_bias.reshape(hid), grad_second)


def solution(mesh):
    spec = P(AXES, None)
    in_specs = (spec, spec, P(AXES, None, None), spec, P(AXES), P(AXES), P(), P(), P())
    out_specs = (spec, spec, P(), P(), P())
    return jax.shard_map(local, mesh=mesh, in_specs=in_specs, out_specs=out_specs, check_vma=False)
```

```python
import functools

import jax
import jax.numpy as jnp
from jax import lax
from jax.experimental import pallas as pl
from jax.experimental.pallas import tpu as pltpu
from jax.sharding import PartitionSpec as P

AXES = ("phi", "eta")
F32 = jnp.float32
BF16 = jnp.bfloat16
VMEM_LIMIT = 60 * 1024 * 1024


def dot(a, b):
    return jnp.dot(a, b, preferred_element_type=F32)


def dot_nt(a, b):
    return lax.dot_general(a, b, (((1,), (1,)), ((), ())), preferred_element_type=F32)


def dot_tn(a, b):
    return lax.dot_general(a, b, (((0,), (0,)), ((), ())), preferred_element_type=F32)


def pick_rows(idx, n):
    t = idx.shape[1]
    cols = jnp.broadcast_to(idx, (128, t)).T
    lane = lax.broadcasted_iota(jnp.int32, (t, 128), 1)
    parts = [jnp.where(cols - 128 * j == lane, 1.0, 0.0).astype(BF16) for j in range(n // 128)]
    return jnp.concatenate(parts, axis=1)


def pick_cols(idx, n, start=0):
    row = lax.broadcasted_iota(jnp.int32, (n, idx.shape[1]), 0)
    return jnp.where(row == idx - start, 1.0, 0.0).astype(BF16)


MESH = pl.DeviceIdType.MESH


def place(n_phi, n_eta):
    phi = lax.axis_index("phi")
    eta = lax.axis_index("eta")
    return phi, eta, phi * n_eta + eta, n_phi * n_eta


def greet_all(n_eta, me, ndev):
    barrier = pltpu.get_barrier_semaphore()

    def greet(k, carry):
        peer = lax.rem(me + k, ndev)
        pl.semaphore_signal(
            barrier, inc=1, device_id=(peer // n_eta, lax.rem(peer, n_eta)), device_id_type=MESH
        )
        return carry

    lax.fori_loop(1, ndev, greet, 0)
    return barrier


def exchange(n_eta, me, ndev, k, src, dst, send_sem, recv_sem):
    peer = lax.rem(me + k, ndev)
    return pltpu.make_async_remote_copy(
        src_ref=src(peer),
        dst_ref=dst(me),
        send_sem=send_sem.at[k],
        recv_sem=recv_sem.at[k],
        device_id=(peer // n_eta, lax.rem(peer, n_eta)),
        device_id_type=MESH,
    )


def near_kernel(
    n_phi, n_eta, loc_ref, rows_ref, edges_ref, cot_ref, near_ref, arr_ref,
    ec, outbox, inbox, send_sem, recv_sem,
):
    step = pl.program_id(0)
    width = edges_ref.shape[1]
    phi, eta, me, ndev = place(n_phi, n_eta)
    cap = outbox.shape[1]
    copy_of = lambda k: exchange(
        n_eta, me, ndev, k, lambda d: outbox.at[d], lambda d: inbox.at[d], send_sem, recv_sem
    )

    @pl.when(step == 0)
    def _():
        barrier = greet_all(n_eta, me, ndev)
        ec[:, :width] = edges_ref[...]
        ec[:, width:] = cot_ref[...]
        slots = ndev * cap
        part = slots if slots < 1024 else 1024
        for p in range(slots // part):
            rows = rows_ref[:, p * part : (p + 1) * part]
            picked = dot(pick_rows(rows, ec.shape[0]), ec[...]).astype(BF16)
            outbox[p * part // cap : (p + 1) * part // cap] = picked.reshape(part // cap, cap, 2 * width)
        inbox[me] = outbox[me]
        pl.semaphore_wait(barrier, ndev - 1)

        def send(k, carry):
            copy_of(k).start()
            return carry

        lax.fori_loop(1, ndev, send, 0)

    near_ref[...] = dot(pick_rows(loc_ref[0], ec.shape[0]), ec[...]).astype(BF16)

    @pl.when(step == pl.num_programs(0) - 1)
    def _():
        def settle(k, carry):
            copy_of(k).wait()
            return carry

        lax.fori_loop(1, ndev, settle, 0)
        arr_ref[...] = inbox[...]


def main_kernel(
    fused, rem_ref, near_ref, arr_ref, w1_ref, b1_ref, w2_ref,
    mda_ref, slot_ref, grad_ref, bias_ref,
    acc_r, g1, g2,
):
    step = pl.program_id(0)
    width = w2_ref.shape[1]
    slots_n = arr_ref.shape[0]

    @pl.when(step == 0)
    def _():
        acc_r[...] = jnp.zeros_like(acc_r)
        g1[...] = jnp.zeros_like(g1)
        g2[...] = jnp.zeros_like(g2)
        bias_ref[...] = jnp.zeros_like(bias_ref)

    rem = rem_ref[0]
    far = dot(pick_rows(rem, slots_n), arr_ref[...])
    a_b = near_ref[:, :width]
    a = a_b.astype(F32)
    b = far[:, :width]
    dm = (near_ref[:, width:].astype(F32) + far[:, width:]).astype(BF16)
    x = jnp.concatenate([a_b, b.astype(BF16), (a * b).astype(BF16)], axis=1)
    pre = dot(x, w1_ref[...]) + b1_ref[...]
    sig = 0.5 * jnp.tanh(0.5 * pre) + 0.5
    h = (pre * sig).astype(BF16)
    m = dot(h, w2_ref[...]).astype(BF16)
    dpre = dot_nt(dm, w2_ref[...]) * (sig * (1.0 + pre * (1.0 - sig)))
    dpre_b = dpre.astype(BF16)
    dx = dot_nt(dpre_b, w1_ref[...])
    dprod = dx[:, 2 * width :]
    mda_ref[:, :width] = m
    mda_ref[:, width:] = (dx[:, :width] + dprod * b).astype(BF16)
    db = (dx[:, width : 2 * width] + dprod * a).astype(BF16)
    g1[...] += dot_tn(x, dpre_b)
    g2[...] += dot_tn(h, dm)
    bias_ref[...] += jnp.sum(dpre, axis=0, keepdims=True)
    acc_r[...] += dot(pick_cols(rem, slots_n), jnp.concatenate([m, db], axis=1))

    @pl.when(step == pl.num_programs(0) - 1)
    def _():
        second = jnp.concatenate(
            [g2[k * width : (k + 1) * width, :] for k in range(g2.shape[0] // width)], axis=1
        )
        if fused:
            ndev, both, wide = slot_ref.shape
            cap = slots_n // ndev
            share = both - cap
            slot_ref[:, :cap, :] = acc_r[...].astype(BF16).reshape(ndev, cap, wide)
            split = g1.shape[0] // share
            slot_ref[:split, cap:, :] = g1[...].astype(BF16).reshape(split, share, wide)
            slot_ref[split:, cap:, :] = second.astype(BF16).reshape(ndev - split, share, wide)
            grad_ref[...] = jnp.zeros_like(grad_ref)
        else:
            n_in = g1.shape[0]
            slot_ref[...] = acc_r[...].astype(BF16)
            grad_ref[:n_in, :] = g1[...].astype(BF16)
            grad_ref[n_in:, :] = second.astype(BF16)


def scatter_kernel(
    n_phi, n_eta, loc_ref, mda_ref, pay_ref, bias_ref,
    sum_ref, back_ref, out_ref, outb_ref,
    shares, inbox, buf, bufb,
    send_g, recv_g, send_s, recv_s, send_a, recv_a, send_b, recv_b,
):
    step = pl.program_id(0)
    last = pl.num_programs(0) - 1
    phi, eta, me, ndev = place(n_phi, n_eta)
    cap = inbox.shape[1]
    share = buf.shape[1]
    pairs = n_phi // 2
    row = [(phi, lax.rem(eta + k, n_eta)) for k in range(1, n_eta)]
    column = [(lax.rem(phi + 2 * k, n_phi), eta) for k in range(1, pairs)]
    mate = (phi + 1 - 2 * lax.rem(phi, 2), eta)
    own = lax.rem(phi, 2)
    stages = [
        [(peer, me, 1) for peer in row],
        [(peer, phi * n_eta, n_eta) for peer in column],
        [(mate, (own + 2 * k) * n_eta, n_eta) for k in range(pairs)],
    ]
    bases = [0, len(row), len(row) + len(column)]

    def grad_copy(k):
        return exchange(
            n_eta, me, ndev, k,
            lambda d: pay_ref.at[d, pl.ds(cap, share)], lambda d: shares.at[d], send_g, recv_g,
        )

    def slot_copy(k):
        return exchange(
            n_eta, me, ndev, k,
            lambda d: pay_ref.at[d, pl.ds(0, cap)], lambda d: inbox.at[d], send_s, recv_s,
        )

    def each(first, end, act):
        def body(k, carry):
            act(k)
            return carry

        lax.fori_loop(first, end, body, 0)

    def stage_copies(stage):
        copies = []
        for n, (peer, start, count) in enumerate(stages[stage]):
            slot = bases[stage] + n
            for data, sends, recvs in ((buf, send_a, recv_a), (bufb, send_b, recv_b)):
                part = data.at[pl.ds(start, count)]
                copies.append(
                    pltpu.make_async_remote_copy(
                        src_ref=part,
                        dst_ref=part,
                        send_sem=sends.at[slot],
                        recv_sem=recvs.at[slot],
                        device_id=peer,
                        device_id_type=MESH,
                    )
                )
        return copies

    def begin(stage):
        for copy in stage_copies(stage):
            copy.start()

    def finish(stage):
        for copy in stage_copies(stage):
            copy.wait()

    cut1, cut2 = 1 + (ndev - 1) // 3, 1 + 2 * (ndev - 1) // 3

    @pl.when(step == 0)
    def _():
        barrier = greet_all(n_eta, me, ndev)
        sum_ref[...] = jnp.zeros_like(sum_ref)
        bufb[me] = bias_ref[...]
        shares[me] = pay_ref[me, cap:, :]
        inbox[me] = pay_ref[me, :cap, :]
        pl.semaphore_wait(barrier, ndev - 1)
        each(1, ndev, lambda k: grad_copy(k).start())
        each(1, cut1, lambda k: slot_copy(k).start())

    @pl.when(step == last // 2)
    def _():
        each(1, ndev, lambda k: grad_copy(k).wait())
        buf[me] = jnp.sum(shares[...].astype(F32), axis=0).astype(BF16)

    sum_ref[...] += dot(pick_cols(loc_ref[0], sum_ref.shape[0]), mda_ref[...])

    @pl.when(step == last // 2)
    def _():
        begin(0)
        each(cut1, cut2, lambda k: slot_copy(k).start())

    @pl.when(step == last * 3 // 4)
    def _():
        finish(0)
        begin(1)
        each(cut2, ndev, lambda k: slot_copy(k).start())

    @pl.when(step == last)
    def _():
        finish(1)
        begin(2)
        each(1, ndev, lambda k: slot_copy(k).wait())
        back_ref[...] = inbox[...]
        finish(2)
        out_ref[...] = buf[...]
        outb_ref[...] = bufb[...]


def final_kernel(
    rows_ref, back_ref, local_ref, edges_ref, cot_ref, pack_ref, bias_ref,
    new_ref, grad_ref, g1_ref, g2_ref, gb_ref,
):
    tile, width = edges_ref.shape
    ndev = back_ref.shape[0]
    slots = rows_ref.shape[1]
    hot = pick_cols(rows_ref[...], tile, pl.program_id(0) * tile)
    returned = back_ref[...].reshape(slots, 2 * width)
    total = local_ref[...] + dot(hot, returned)
    new_ref[...] = (edges_ref[...].astype(F32) + total[:, :width]).astype(BF16)
    grad_ref[...] = (cot_ref[...].astype(F32) + total[:, width:]).astype(BF16)

    @pl.when(pl.program_id(0) == 0)
    def _():
        n_in = g1_ref.shape[0]
        g1_ref[...] = pack_ref[:n_in, :].astype(F32)
        for k in range(g2_ref.shape[0] // width):
            g2_ref[k * width : (k + 1) * width, :] = pack_ref[n_in:, k * width : (k + 1) * width].astype(F32)
        gb_ref[...] = jnp.sum(bias_ref[...], axis=0)


def full(shape):
    return pl.BlockSpec(shape, lambda i: (0,) * len(shape))


def params():
    return pltpu.CompilerParams(dimension_semantics=("arbitrary",), vmem_limit_bytes=VMEM_LIMIT)


def tile_of(n, want):
    return want if n % want == 0 else n


def local(
    edges, cotangent, send_rows, send_count, trip_local, trip_remote, w_first, bias_first, w_second
):
    n_edges, width = edges.shape
    n_in, hid = w_first.shape
    ndev = lax.axis_size("phi") * lax.axis_size("eta")
    cap = send_rows.shape[2]
    slots = ndev * cap
    n_trip = trip_local.shape[0]
    live = jnp.arange(cap, dtype=jnp.int32)[None, :] < send_count[0][:, None]
    rows = jnp.where(live, send_rows[0], -1)

    tt = tile_of(n_trip, 1024)
    steps = n_trip // tt
    wide = 2 * width
    pack = n_in + width
    share = pack // ndev
    loc = trip_local.reshape(steps, 1, tt)
    rem = trip_remote.reshape(steps, 1, tt)
    idx_block = pl.BlockSpec((1, 1, tt), lambda i: (i, 0, 0))
    trip_block = pl.BlockSpec((tt, wide), lambda i: (i, 0))
    n_phi, n_eta = lax.axis_size("phi"), lax.axis_size("eta")
    flat = rows.reshape(1, slots)
    remote = lambda n: pltpu.CompilerParams(
        dimension_semantics=("arbitrary",),
        collective_id=n,
        has_side_effects=True,
        vmem_limit_bytes=VMEM_LIMIT,
    )
    box = pltpu.VMEM((ndev, cap, wide), BF16)
    each_dev = pltpu.SemaphoreType.DMA((ndev,))
    near, arrived = pl.pallas_call(
        functools.partial(near_kernel, n_phi, n_eta),
        grid=(steps,),
        in_specs=[idx_block, full((1, slots)), full((n_edges, width)), full((n_edges, width))],
        out_specs=[trip_block, full((ndev, cap, wide))],
        out_shape=[
            jax.ShapeDtypeStruct((n_trip, wide), BF16),
            jax.ShapeDtypeStruct((ndev, cap, wide), BF16),
        ],
        scratch_shapes=[pltpu.VMEM((n_edges, wide), BF16), box, box, each_dev, each_dev],
        compiler_params=remote(0),
        name="near_rows",
    )(loc, flat, edges, cotangent)
    arrived = arrived.reshape(slots, wide)

    fused = share % 16 == 0 and n_in % share == 0 and cap % 16 == 0
    if fused:
        slot_shape, grad_shape = (ndev, cap + share, wide), (8, hid)
    else:
        slot_shape, grad_shape = (slots, wide), (pack, hid)
    mda, payload, grads, bias = pl.pallas_call(
        functools.partial(main_kernel, fused),
        grid=(steps,),
        in_specs=[
            idx_block,
            trip_block,
            full((slots, wide)),
            full((n_in, hid)),
            full((1, hid)),
            full((hid, width)),
        ],
        out_specs=[trip_block, full(slot_shape), full(grad_shape), full((1, hid))],
        out_shape=[
            jax.ShapeDtypeStruct((n_trip, wide), BF16),
            jax.ShapeDtypeStruct(slot_shape, BF16),
            jax.ShapeDtypeStruct(grad_shape, BF16),
            jax.ShapeDtypeStruct((1, hid), F32),
        ],
        scratch_shapes=[
            pltpu.VMEM((slots, wide), F32),
            pltpu.VMEM((n_in, hid), F32),
            pltpu.VMEM((hid, width), F32),
        ],
        compiler_params=params(),
        cost_estimate=pl.CostEstimate(
            flops=12 * n_trip * n_in * hid, bytes_accessed=8 * n_trip * wide, transcendentals=0
        ),
        name="triplets",
    )(rem, near, arrived, w_first, bias_first.reshape(1, hid), w_second)
    if not fused:
        payload = jnp.concatenate(
            [payload.reshape(ndev, cap, wide), grads.reshape(ndev, share, hid)], axis=1
        )
    moves = n_eta - 1 + n_phi // 2 - 1 + n_phi // 2
    sems = pltpu.SemaphoreType.DMA((moves,))
    near_sum, back, packed, biases = pl.pallas_call(
        functools.partial(scatter_kernel, n_phi, n_eta),
        grid=(steps,),
        in_specs=[idx_block, trip_block, full((ndev, cap + share, wide)), full((1, hid))],
        out_specs=[
            full((n_edges, wide)),
            full((ndev, cap, wide)),
            full((ndev, share, hid)),
            full((ndev, 1, hid)),
        ],
        out_shape=[
            jax.ShapeDtypeStruct((n_edges, wide), F32),
            jax.ShapeDtypeStruct((ndev, cap, wide), BF16),
            jax.ShapeDtypeStruct((ndev, share, hid), BF16),
            jax.ShapeDtypeStruct((ndev, 1, hid), F32),
        ],
        scratch_shapes=[
            pltpu.VMEM((ndev, share, hid), BF16),
            box,
            pltpu.VMEM((ndev, share, hid), BF16),
            pltpu.VMEM((ndev, 1, hid), F32),
        ]
        + [each_dev] * 4
        + [sems] * 4,
        compiler_params=remote(1),
        name="near_sum",
    )(loc, mda, payload, bias)

    et = tile_of(n_edges, 512)
    row_block = lambda w: pl.BlockSpec((et, w), lambda i: (i, 0))
    new_edges, edge_grad, grad_first, grad_second, grad_bias = pl.pallas_call(
        final_kernel,
        grid=(n_edges // et,),
        in_specs=[
            full((1, slots)),
            full((ndev, cap, wide)),
            row_block(wide),
            row_block(width),
            row_block(width),
            full((pack, hid)),
            full((ndev, 1, hid)),
        ],
        out_specs=[
            row_block(width),
            row_block(width),
            full((n_in, hid)),
            full((hid, width)),
            full((1, hid)),
        ],
        out_shape=[
            jax.ShapeDtypeStruct((n_edges, width), BF16),
            jax.ShapeDtypeStruct((n_edges, width), BF16),
            jax.ShapeDtypeStruct((n_in, hid), F32),
            jax.ShapeDtypeStruct((hid, width), F32),
            jax.ShapeDtypeStruct((1, hid), F32),
        ],
        compiler_params=params(),
        name="add_up",
    )(flat, back, near_sum, edges, cotangent, packed.reshape(pack, hid), biases)
    return (new_edges, edge_grad, grad_first, grad_bias.reshape(hid), grad_second)


def solution(mesh):
    spec = P(AXES, None)
    in_specs = (spec, spec, P(AXES, None, None), spec, P(AXES), P(AXES), P(), P(), P())
    out_specs = (spec, spec, P(), P(), P())
    return jax.shard_map(local, mesh=mesh, in_specs=in_specs, out_specs=out_specs, check_vma=False)
```

```python
import functools

import jax
import jax.numpy as jnp
from jax import lax
from jax.experimental import pallas as pl
from jax.experimental.pallas import tpu as pltpu
from jax.sharding import PartitionSpec as P

AXES = ("phi", "eta")
F32 = jnp.float32
BF16 = jnp.bfloat16
TM = 512
VMEM_LIMIT = 60 * 1024 * 1024


def dot(a, b):
    return jnp.dot(a, b, preferred_element_type=F32)


def dot_nt(a, b):
    return lax.dot_general(a, b, (((1,), (1,)), ((), ())), preferred_element_type=F32)


def dot_tn(a, b):
    return lax.dot_general(a, b, (((0,), (0,)), ((), ())), preferred_element_type=F32)


def pick_rows(idx, n):
    t = idx.shape[1]
    cols = jnp.broadcast_to(idx, (128, t)).T
    lane = lax.broadcasted_iota(jnp.int32, (t, 128), 1)
    parts = [jnp.where(cols - 128 * j == lane, 1.0, 0.0).astype(BF16) for j in range(n // 128)]
    return jnp.concatenate(parts, axis=1)


def pick_cols(idx, n, start=0):
    row = lax.broadcasted_iota(jnp.int32, (n, idx.shape[1]), 0)
    return jnp.where(row == idx - start, 1.0, 0.0).astype(BF16)


MESH = pl.DeviceIdType.MESH


def place(n_phi, n_eta):
    phi = lax.axis_index("phi")
    eta = lax.axis_index("eta")
    return phi, eta, phi * n_eta + eta, n_phi * n_eta


def greet_all(n_eta, me, ndev):
    barrier = pltpu.get_barrier_semaphore()

    def greet(k, carry):
        peer = lax.rem(me + k, ndev)
        pl.semaphore_signal(
            barrier, inc=1, device_id=(peer // n_eta, lax.rem(peer, n_eta)), device_id_type=MESH
        )
        return carry

    lax.fori_loop(1, ndev, greet, 0)
    return barrier


def exchange(n_eta, me, ndev, k, src, dst, send_sem, recv_sem):
    peer = lax.rem(me + k, ndev)
    return pltpu.make_async_remote_copy(
        src_ref=src(peer),
        dst_ref=dst(me),
        send_sem=send_sem.at[k],
        recv_sem=recv_sem.at[k],
        device_id=(peer // n_eta, lax.rem(peer, n_eta)),
        device_id_type=MESH,
    )


def near_kernel(
    n_phi, n_eta, loc_ref, rows_ref, edges_ref, cot_ref, near_ref, arr_ref,
    ec, outbox, inbox, send_sem, recv_sem,
):
    step = pl.program_id(0)
    width = edges_ref.shape[1]
    phi, eta, me, ndev = place(n_phi, n_eta)
    cap = outbox.shape[1]
    copy_of = lambda k: exchange(
        n_eta, me, ndev, k, lambda d: outbox.at[d], lambda d: inbox.at[d], send_sem, recv_sem
    )

    @pl.when(step == 0)
    def _():
        barrier = greet_all(n_eta, me, ndev)
        ec[:, :width] = edges_ref[...]
        ec[:, width:] = cot_ref[...]
        slots = ndev * cap
        part = slots if slots < 1024 else 1024
        for p in range(slots // part):
            rows = rows_ref[:, p * part : (p + 1) * part]
            picked = dot(pick_rows(rows, ec.shape[0]), ec[...]).astype(BF16)
            outbox[p * part // cap : (p + 1) * part // cap] = picked.reshape(part // cap, cap, 2 * width)
        inbox[me] = outbox[me]
        pl.semaphore_wait(barrier, ndev - 1)

        def send(k, carry):
            copy_of(k).start()
            return carry

        lax.fori_loop(1, ndev, send, 0)

    near_ref[...] = dot(pick_rows(loc_ref[0], ec.shape[0]), ec[...]).astype(BF16)

    @pl.when(step == pl.num_programs(0) - 1)
    def _():
        def settle(k, carry):
            copy_of(k).wait()
            return carry

        lax.fori_loop(1, ndev, settle, 0)
        arr_ref[...] = inbox[...]


def main_kernel(
    fused, rem_ref, near_ref, arr_ref, w1_ref, b1_ref, w2_ref,
    mda_ref, slot_ref, grad_ref, bias_ref,
    acc_r, g1, g2,
):
    step = pl.program_id(0)
    width = w2_ref.shape[1]
    slots_n = arr_ref.shape[0]

    @pl.when(step == 0)
    def _():
        acc_r[...] = jnp.zeros_like(acc_r)
        g1[...] = jnp.zeros_like(g1)
        g2[...] = jnp.zeros_like(g2)
        bias_ref[...] = jnp.zeros_like(bias_ref)

    rem = rem_ref[0]
    far = dot(pick_rows(rem, slots_n), arr_ref[...])
    a_b = near_ref[:, :width]
    a = a_b.astype(F32)
    b = far[:, :width]
    dm = (near_ref[:, width:].astype(F32) + far[:, width:]).astype(BF16)
    x = jnp.concatenate([a_b, b.astype(BF16), (a * b).astype(BF16)], axis=1)
    pre = dot(x, w1_ref[...]) + b1_ref[...]
    sig = 0.5 * jnp.tanh(0.5 * pre) + 0.5
    h = (pre * sig).astype(BF16)
    m = dot(h, w2_ref[...]).astype(BF16)
    dpre = dot_nt(dm, w2_ref[...]) * (sig * (1.0 + pre * (1.0 - sig)))
    dpre_b = dpre.astype(BF16)
    dx = dot_nt(dpre_b, w1_ref[...])
    dprod = dx[:, 2 * width :]
    mda_ref[:, :width] = m
    mda_ref[:, width:] = (dx[:, :width] + dprod * b).astype(BF16)
    db = (dx[:, width : 2 * width] + dprod * a).astype(BF16)
    g1[...] += dot_tn(x, dpre_b)
    g2[...] += dot_tn(h, dm)
    bias_ref[...] += jnp.sum(dpre, axis=0, keepdims=True)
    acc_r[...] += dot(pick_cols(rem, slots_n), jnp.concatenate([m, db], axis=1))

    @pl.when(step == pl.num_programs(0) - 1)
    def _():
        second = jnp.concatenate(
            [g2[k * width : (k + 1) * width, :] for k in range(g2.shape[0] // width)], axis=1
        )
        if fused:
            ndev, both, wide = slot_ref.shape
            cap = slots_n // ndev
            share = both - cap
            slot_ref[:, :cap, :] = acc_r[...].astype(BF16).reshape(ndev, cap, wide)
            split = g1.shape[0] // share
            slot_ref[:split, cap:, :] = g1[...].astype(BF16).reshape(split, share, wide)
            slot_ref[split:, cap:, :] = second.astype(BF16).reshape(ndev - split, share, wide)
            grad_ref[...] = jnp.zeros_like(grad_ref)
        else:
            n_in = g1.shape[0]
            slot_ref[...] = acc_r[...].astype(BF16)
            grad_ref[:n_in, :] = g1[...].astype(BF16)
            grad_ref[n_in:, :] = second.astype(BF16)


def scatter_kernel(
    n_phi, n_eta, loc_ref, mda_ref, pay_ref, bias_ref,
    sum_ref, back_ref, out_ref, outb_ref,
    shares, inbox, buf, bufb,
    send_g, recv_g, send_s, recv_s, send_a, recv_a, send_b, recv_b,
):
    step = pl.program_id(0)
    last = pl.num_programs(0) - 1
    phi, eta, me, ndev = place(n_phi, n_eta)
    cap = inbox.shape[1]
    share = buf.shape[1]
    pairs = n_phi // 2
    row = [(phi, lax.rem(eta + k, n_eta)) for k in range(1, n_eta)]
    column = [(lax.rem(phi + 2 * k, n_phi), eta) for k in range(1, pairs)]
    mate = (phi + 1 - 2 * lax.rem(phi, 2), eta)
    own = lax.rem(phi, 2)
    stages = [
        [(peer, me, 1) for peer in row],
        [(peer, phi * n_eta, n_eta) for peer in column],
        [(mate, (own + 2 * k) * n_eta, n_eta) for k in range(pairs)],
    ]
    bases = [0, len(row), len(row) + len(column)]

    def grad_copy(k):
        return exchange(
            n_eta, me, ndev, k,
            lambda d: pay_ref.at[d, pl.ds(cap, share)], lambda d: shares.at[d], send_g, recv_g,
        )

    def slot_copy(k):
        return exchange(
            n_eta, me, ndev, k,
            lambda d: pay_ref.at[d, pl.ds(0, cap)], lambda d: inbox.at[d], send_s, recv_s,
        )

    def each(first, end, act):
        def body(k, carry):
            act(k)
            return carry

        lax.fori_loop(first, end, body, 0)

    def stage_copies(stage):
        copies = []
        for n, (peer, start, count) in enumerate(stages[stage]):
            slot = bases[stage] + n
            for data, sends, recvs in ((buf, send_a, recv_a), (bufb, send_b, recv_b)):
                part = data.at[pl.ds(start, count)]
                copies.append(
                    pltpu.make_async_remote_copy(
                        src_ref=part,
                        dst_ref=part,
                        send_sem=sends.at[slot],
                        recv_sem=recvs.at[slot],
                        device_id=peer,
                        device_id_type=MESH,
                    )
                )
        return copies

    def begin(stage):
        for copy in stage_copies(stage):
            copy.start()

    def finish(stage):
        for copy in stage_copies(stage):
            copy.wait()

    cut1, cut2 = 1 + (ndev - 1) // 3, 1 + 2 * (ndev - 1) // 3

    @pl.when(step == 0)
    def _():
        barrier = greet_all(n_eta, me, ndev)
        sum_ref[...] = jnp.zeros_like(sum_ref)
        bufb[me] = bias_ref[...]
        shares[me] = pay_ref[me, cap:, :]
        inbox[me] = pay_ref[me, :cap, :]
        pl.semaphore_wait(barrier, ndev - 1)
        each(1, ndev, lambda k: grad_copy(k).start())
        each(1, cut1, lambda k: slot_copy(k).start())

    @pl.when(step == last // 2)
    def _():
        each(1, ndev, lambda k: grad_copy(k).wait())
        buf[me] = jnp.sum(shares[...].astype(F32), axis=0).astype(BF16)

    sum_ref[...] += dot(pick_cols(loc_ref[0], sum_ref.shape[0]), mda_ref[...])

    @pl.when(step == last // 2)
    def _():
        begin(0)
        each(cut1, cut2, lambda k: slot_copy(k).start())

    @pl.when(step == last * 3 // 4)
    def _():
        finish(0)
        begin(1)
        each(cut2, ndev, lambda k: slot_copy(k).start())

    @pl.when(step == last)
    def _():
        finish(1)
        begin(2)
        each(1, ndev, lambda k: slot_copy(k).wait())
        back_ref[...] = inbox[...]
        finish(2)
        out_ref[...] = buf[...]
        outb_ref[...] = bufb[...]


def final_kernel(
    rows_ref, back_ref, local_ref, edges_ref, cot_ref, pack_ref, bias_ref,
    new_ref, grad_ref, g1_ref, g2_ref, gb_ref,
):
    tile, width = edges_ref.shape
    ndev = back_ref.shape[0]
    slots = rows_ref.shape[1]
    hot = pick_cols(rows_ref[...], tile, pl.program_id(0) * tile)
    returned = back_ref[...].reshape(slots, 2 * width)
    total = local_ref[...] + dot(hot, returned)
    new_ref[...] = (edges_ref[...].astype(F32) + total[:, :width]).astype(BF16)
    grad_ref[...] = (cot_ref[...].astype(F32) + total[:, width:]).astype(BF16)

    @pl.when(pl.program_id(0) == 0)
    def _():
        n_in = g1_ref.shape[0]
        g1_ref[...] = pack_ref[:n_in, :].astype(F32)
        for k in range(g2_ref.shape[0] // width):
            g2_ref[k * width : (k + 1) * width, :] = pack_ref[n_in:, k * width : (k + 1) * width].astype(F32)
        gb_ref[...] = jnp.sum(bias_ref[...], axis=0)


def full(shape):
    return pl.BlockSpec(shape, lambda i: (0,) * len(shape))


def params():
    return pltpu.CompilerParams(dimension_semantics=("arbitrary",), vmem_limit_bytes=VMEM_LIMIT)


def tile_of(n, want):
    return want if n % want == 0 else n


def local(
    edges, cotangent, send_rows, send_count, trip_local, trip_remote, w_first, bias_first, w_second
):
    n_edges, width = edges.shape
    n_in, hid = w_first.shape
    ndev = lax.axis_size("phi") * lax.axis_size("eta")
    cap = send_rows.shape[2]
    slots = ndev * cap
    n_trip = trip_local.shape[0]
    live = jnp.arange(cap, dtype=jnp.int32)[None, :] < send_count[0][:, None]
    rows = jnp.where(live, send_rows[0], -1)

    tt = tile_of(n_trip, 1024)
    steps = n_trip // tt
    wide = 2 * width
    pack = n_in + width
    share = pack // ndev
    loc = trip_local.reshape(steps, 1, tt)
    tm = tile_of(n_trip, TM)
    rem = trip_remote.reshape(n_trip // tm, 1, tm)
    idx_block = pl.BlockSpec((1, 1, tt), lambda i: (i, 0, 0))
    trip_block = pl.BlockSpec((tt, wide), lambda i: (i, 0))
    n_phi, n_eta = lax.axis_size("phi"), lax.axis_size("eta")
    flat = rows.reshape(1, slots)
    remote = lambda n: pltpu.CompilerParams(
        dimension_semantics=("arbitrary",),
        collective_id=n,
        has_side_effects=True,
        vmem_limit_bytes=VMEM_LIMIT,
    )
    box = pltpu.VMEM((ndev, cap, wide), BF16)
    each_dev = pltpu.SemaphoreType.DMA((ndev,))
    near, arrived = pl.pallas_call(
        functools.partial(near_kernel, n_phi, n_eta),
        grid=(steps,),
        in_specs=[idx_block, full((1, slots)), full((n_edges, width)), full((n_edges, width))],
        out_specs=[trip_block, full((ndev, cap, wide))],
        out_shape=[
            jax.ShapeDtypeStruct((n_trip, wide), BF16),
            jax.ShapeDtypeStruct((ndev, cap, wide), BF16),
        ],
        scratch_shapes=[pltpu.VMEM((n_edges, wide), BF16), box, box, each_dev, each_dev],
        compiler_params=remote(0),
        name="near_rows",
    )(loc, flat, edges, cotangent)
    arrived = arrived.reshape(slots, wide)

    fused = share % 16 == 0 and n_in % share == 0 and cap % 16 == 0
    if fused:
        slot_shape, grad_shape = (ndev, cap + share, wide), (8, hid)
    else:
        slot_shape, grad_shape = (slots, wide), (pack, hid)
    mda, payload, grads, bias = pl.pallas_call(
        functools.partial(main_kernel, fused),
        grid=(n_trip // tm,),
        in_specs=[
            pl.BlockSpec((1, 1, tm), lambda i: (i, 0, 0)),
            pl.BlockSpec((tm, wide), lambda i: (i, 0)),
            full((slots, wide)),
            full((n_in, hid)),
            full((1, hid)),
            full((hid, width)),
        ],
        out_specs=[pl.BlockSpec((tm, wide), lambda i: (i, 0)), full(slot_shape), full(grad_shape), full((1, hid))],
        out_shape=[
            jax.ShapeDtypeStruct((n_trip, wide), BF16),
            jax.ShapeDtypeStruct(slot_shape, BF16),
            jax.ShapeDtypeStruct(grad_shape, BF16),
            jax.ShapeDtypeStruct((1, hid), F32),
        ],
        scratch_shapes=[
            pltpu.VMEM((slots, wide), F32),
            pltpu.VMEM((n_in, hid), F32),
            pltpu.VMEM((hid, width), F32),
        ],
        compiler_params=params(),
        cost_estimate=pl.CostEstimate(
            flops=12 * n_trip * n_in * hid, bytes_accessed=8 * n_trip * wide, transcendentals=0
        ),
        name="triplets",
    )(rem, near, arrived, w_first, bias_first.reshape(1, hid), w_second)
    if not fused:
        payload = jnp.concatenate(
            [payload.reshape(ndev, cap, wide), grads.reshape(ndev, share, hid)], axis=1
        )
    moves = n_eta - 1 + n_phi // 2 - 1 + n_phi // 2
    sems = pltpu.SemaphoreType.DMA((moves,))
    near_sum, back, packed, biases = pl.pallas_call(
        functools.partial(scatter_kernel, n_phi, n_eta),
        grid=(steps,),
        in_specs=[idx_block, trip_block, full((ndev, cap + share, wide)), full((1, hid))],
        out_specs=[
            full((n_edges, wide)),
            full((ndev, cap, wide)),
            full((ndev, share, hid)),
            full((ndev, 1, hid)),
        ],
        out_shape=[
            jax.ShapeDtypeStruct((n_edges, wide), F32),
            jax.ShapeDtypeStruct((ndev, cap, wide), BF16),
            jax.ShapeDtypeStruct((ndev, share, hid), BF16),
            jax.ShapeDtypeStruct((ndev, 1, hid), F32),
        ],
        scratch_shapes=[
            pltpu.VMEM((ndev, share, hid), BF16),
            box,
            pltpu.VMEM((ndev, share, hid), BF16),
            pltpu.VMEM((ndev, 1, hid), F32),
        ]
        + [each_dev] * 4
        + [sems] * 4,
        compiler_params=remote(1),
        name="near_sum",
    )(loc, mda, payload, bias)

    et = tile_of(n_edges, 512)
    row_block = lambda w: pl.BlockSpec((et, w), lambda i: (i, 0))
    new_edges, edge_grad, grad_first, grad_second, grad_bias = pl.pallas_call(
        final_kernel,
        grid=(n_edges // et,),
        in_specs=[
            full((1, slots)),
            full((ndev, cap, wide)),
            row_block(wide),
            row_block(width),
            row_block(width),
            full((pack, hid)),
            full((ndev, 1, hid)),
        ],
        out_specs=[
            row_block(width),
            row_block(width),
            full((n_in, hid)),
            full((hid, width)),
            full((1, hid)),
        ],
        out_shape=[
            jax.ShapeDtypeStruct((n_edges, width), BF16),
            jax.ShapeDtypeStruct((n_edges, width), BF16),
            jax.ShapeDtypeStruct((n_in, hid), F32),
            jax.ShapeDtypeStruct((hid, width), F32),
            jax.ShapeDtypeStruct((1, hid), F32),
        ],
        compiler_params=params(),
        name="add_up",
    )(flat, back, near_sum, edges, cotangent, packed.reshape(pack, hid), biases)
    return (new_edges, edge_grad, grad_first, grad_bias.reshape(hid), grad_second)


def solution(mesh):
    spec = P(AXES, None)
    in_specs = (spec, spec, P(AXES, None, None), spec, P(AXES), P(AXES), P(), P(), P())
    out_specs = (spec, spec, P(), P(), P())
    return jax.shard_map(local, mesh=mesh, in_specs=in_specs, out_specs=out_specs, check_vma=False)
```
